32 devices in a mesh: tm: 8 (over z, y), obs: 4 (over x, core).
Axes of the slice: x: 2, y: 2, z: 4, core: 2. Of those that a mesh axis runs over, the one named last changes fastest.
Arguments:
- obs_rows: float32 [256, 768], P(('tm', 'obs')), may hold values from -6 to 6
- obs_owner: int32 [256, 1], P(('tm', 'obs')), may hold values from 0 to 7; in each aligned block of 8 rows (0 to 7, 8 to 15, ...) at most 2 rows name the same one
- obs_member: int32 [256, 1], P(('tm', 'obs')), may hold values from 0 to 7
- prior_diag: float32 [64, 384], P(('tm', 'obs')), may hold values from 1 to 4
- lower_coupling: float32 [64, 384, 384], P(('tm', 'obs')), may hold values from -2 to 2
- tip_coupling: float32 [64, 128, 384], P(('tm', 'obs')), may hold values from -0.095683193 to 0.095683193
- time_rhs: float32 [64, 384], P(('tm', 'obs')), may hold values from -6 to 6
- tip_prior: float32 [128], replicated, may hold values from 0.5 to 2
- tip_rhs: float32 [128], replicated, may hold values from -30 to 30
Outputs:
- reduced_block: float32 [64, 384, 384], P(('tm', 'obs'))
- reduced_lower: float32 [64, 384, 384], P(('tm', 'obs'))
- reduced_tip: float32 [64, 128, 384], P(('tm', 'obs'))
- time_result: float32 [64, 384], P(('tm', 'obs'))
- tip_solution: float32 [128], replicated
The draws below stay inside these ranges and needn't reach their ends.
Inputs may be any that keep to these rules, and one draw needn't show every extreme that they name: `obs_owner`: of the 8 observation blocks of one device, at most 2 name the same owner group, and in every draw some device has an owner group named exactly 2 times.
All inputs are finite; a program needn't handle non-finite values.
Results may differ from the reference program's by a relative error of at most 0.00016.
Values sent between devices are 32-bit elements; how exact they have to be, the bound alone decides.
A program may use at most 64 MiB of HBM per device.

```python
import math
import jax
import jax.numpy as jnp
import numpy as np
from jax import lax

B = 384
K = 128
R = 2
CAP = 2
NT = 64
OB_DEV = 8
N_TM = 8
N_OBS = 4


def draw_tip_coupling(key, part):
    base = jnp.clip(jax.random.normal(key, (NT, K, B), jnp.float32), -5.0, 5.0)
    ramp = 1.0 + 2.0 * jnp.arange(NT, dtype=jnp.float32)[:, None, None] / max(NT - 1, 1)
    return base * ramp / math.sqrt(NT * B)


def touch_ends(entries, stream_key, low, top_value):
    longest = entries.shape.index(max(entries.shape))
    spots = []
    for shift in (0, 1):
        where = [jax.random.randint(jax.random.fold_in(stream_key, axis), (), 0, length) for axis, length in enumerate(entries.shape)]
        where[longest] = (where[longest] + shift) % entries.shape[longest]
        spots.append(tuple(where))
    return entries.at[spots[0]].set(low).at[spots[1]].set(top_value)


def level_of(own_key, extent, pieces, low, high):
    level, own = 1.0, jax.random.fold_in(own_key, 6)
    for position, parts in pieces:
        steps = jnp.exp(jax.random.uniform(jax.random.fold_in(own, position), (parts,), jnp.float32, low / len(pieces), high / len(pieces)))
        level = level * jnp.repeat(steps, extent[position] // parts).reshape([-1 if axis == position else 1 for axis in range(len(extent))])
    return level


def deal_out(key, own, number, rows, amount, top, reach, slope):
    sequence = jax.random.permutation(key, amount)
    heavy_load, common = shares(amount, rows * top, reach, slope, True), shares(amount, rows * top, reach, slope, False)
    places = jnp.arange(amount)

    def named(lengths, turn):
        used = int((lengths > 0).sum())
        fixed = max(1, used // 4)
        shifted = fixed + (places - fixed + turn * (used - fixed)) % max(1, amount - fixed)
        return jnp.zeros((amount,), jnp.int32).at[sequence[jnp.where(places < fixed, places, shifted)]].set(jnp.asarray(lengths, jnp.int32))

    lengths = jnp.where(number % 4 == 0, named(heavy_load, number // 4), named(common, number - number // 4 - 1))
    mixed = jax.random.permutation(jax.random.fold_in(own, 3), amount)
    source_of, taker = mixed[0:amount // 2 * 2:2], mixed[1:amount // 2 * 2:2]
    margin = jnp.minimum(lengths[source_of] - 1, reach - lengths[taker]) // 2
    margin = jnp.where((source_of == sequence[0]) | (taker == sequence[0]) | (lengths[taker] == 0), 0, jnp.maximum(margin, 0))
    shifted = jax.random.randint(jax.random.fold_in(own, 4), (amount // 2,), 0, 1 << 20) % (margin + 1)
    lengths = lengths.at[source_of].add(-shifted).at[taker].add(shifted)
    labels = jnp.searchsorted(jnp.cumsum(lengths), jnp.arange(rows * top), side="right").astype(jnp.int32)
    table = labels.reshape(top, rows).T
    table = table[jax.random.permutation(jax.random.fold_in(own, 1), rows)]
    turn = jax.random.randint(jax.random.fold_in(own, 2), (rows, 1), 0, top)
    return jnp.take_along_axis(table, (jnp.arange(top)[None, :] + turn) % top, axis=1)


def shares(amount, total, limit, lean, full):
    loads = [(1 << 20) // math.isqrt(standing ** lean) + 1 for standing in range(1, amount + 1)]
    largest = limit if full else min(limit, max(-(-total // amount), total * loads[0] // sum(loads)))
    least = 1 if total - largest >= amount - 1 else 0
    given, rest = [largest] + [least] * (amount - 1), total - largest - least * (amount - 1)
    while rest > 0:
        candidates = [i for i in range(1, amount) if given[i] < largest] or [i for i in range(1, amount) if given[i] < limit]
        whole, budget = sum([loads[i] for i in candidates]), rest
        for i in candidates:
            addition = min(limit - given[i], max(1, budget * loads[i] // whole), rest)
            given[i] = given[i] + addition
            rest = rest - addition
    return np.array(given)


def bell_draw(own_key, dims, deviation, limit, shards=(), held_as=jnp.bfloat16):
    gain = level_of(own_key, dims, shards, -0.22, 0.18) if shards else 1.0
    values = jax.random.normal(own_key, dims, jnp.float32) * deviation * gain
    return jnp.minimum(jnp.maximum(values, -limit), limit).astype(held_as)


def setup_inputs(seed: int = 0) -> dict:
    key_list = jax.random.split(jax.random.key(seed), 10)
    obs_rows = bell_draw(key_list[0], (N_TM * N_OBS * OB_DEV, R * B), ((3.0 / (OB_DEV * R)) ** 0.5), 6.0, ((0, 32),), jnp.float32)
    obs_owner_keys = jax.random.split(jax.random.fold_in(key_list[1], 1), (N_TM * N_OBS * OB_DEV) // OB_DEV)
    obs_owner_turns = jax.random.permutation(jax.random.fold_in(key_list[1], 3), (N_TM * N_OBS * OB_DEV) // OB_DEV)
    obs_owner = jax.vmap(lambda own, number: deal_out(jax.random.fold_in(key_list[1], 2), own, number, OB_DEV, N_TM, 1, CAP, 2))(obs_owner_keys, obs_owner_turns).reshape((N_TM * N_OBS * OB_DEV, 1))
    obs_member = touch_ends(jax.random.randint(key_list[2], (N_TM * N_OBS * OB_DEV, 1), 0, 2 * N_OBS), jax.random.fold_in(key_list[2], 1), 0, (2 * N_OBS) - 1).astype(jnp.int32)
    prior_diag = jnp.clip(jnp.exp(math.log(4.0) - 1.3862944 * jax.random.uniform(key_list[3], (NT, B), jnp.float32) ** level_of(key_list[3], (NT, B), ((0, 32),), -0.2, 0.2)), 1.0, 4.0)
    lower_coupling = bell_draw(key_list[4], (NT, B, B), (3.0 / B ** 0.5), 2.0, ((0, 32),), jnp.float32)
    tip_coupling = draw_tip_coupling(jax.random.fold_in(key_list[9], 71), 0)
    time_rhs = bell_draw(key_list[6], (NT, B), 1.0, 6.0, ((0, 32),), jnp.float32)
    tip_prior = jnp.clip(jnp.exp(jax.random.uniform(key_list[7], (K,), jnp.float32, math.log(0.5), math.log(2.0))), 0.5, 2.0)
    tip_rhs = bell_draw(key_list[8], (K,), 5.0, 30.0, (), jnp.float32)
    return {"obs_rows": obs_rows, "obs_owner": obs_owner, "obs_member": obs_member, "prior_diag": prior_diag, "lower_coupling": lower_coupling, "tip_coupling": tip_coupling, "time_rhs": time_rhs, "tip_prior": tip_prior, "tip_rhs": tip_rhs}


FULL_PRECISION = lax.Precision.HIGHEST

def solve_lower(factor, right, transpose=False):
    return lax.linalg.triangular_solve(factor, right, left_side=True, lower=True, transpose_a=transpose)

def reference(obs_rows, obs_owner, obs_member, prior_diag, lower_coupling, tip_coupling, time_rhs, tip_prior, tip_rhs):
    target = (obs_owner[:, 0] * (2 * N_OBS) + obs_member[:, 0]).astype(jnp.int32)
    block_total = obs_rows.shape[0]
    batch_size = 64
    row_batches = obs_rows.reshape(block_total // batch_size, batch_size, R, B)
    target_batches = target.reshape(block_total // batch_size, batch_size)

    def add_blocks(grams, item):
        batch_rows, batch_targets = item
        products = jnp.einsum('jrb,jrc->jbc', batch_rows, batch_rows, precision=FULL_PRECISION)
        return (grams.at[batch_targets].add(products), None)
    grams, _ = lax.scan(add_blocks, jnp.zeros((NT, B, B), jnp.float32), (row_batches, target_batches))
    identity = jnp.eye(B, dtype=jnp.float32)
    blocks_all = grams + prior_diag[:, :, None] * identity
    first_mask = (jnp.arange(NT) == 0)[:, None, None]
    low = jnp.where(first_mask, jnp.zeros_like(lower_coupling), lower_coupling)
    even_blocks = blocks_all[0::2]
    odd_blocks = blocks_all[1::2]
    factor = jnp.linalg.cholesky(even_blocks)
    fill_block = solve_lower(factor, low[0::2])
    tip_side = solve_lower(factor, jnp.swapaxes(tip_coupling[0::2], 1, 2))
    lifted = solve_lower(factor, time_rhs[0::2][:, :, None])[:, :, 0]
    left_cross = solve_lower(factor, jnp.swapaxes(low[1::2], 1, 2))
    right_fill = jnp.concatenate([fill_block[1:], jnp.zeros_like(fill_block[:1])], axis=0)
    right_side = jnp.concatenate([tip_side[1:], jnp.zeros_like(tip_side[:1])], axis=0)
    right_lift = jnp.concatenate([lifted[1:], jnp.zeros_like(lifted[:1])], axis=0)

    def pair_product(left, right):
        return jnp.einsum('ibk,ibc->ikc', left, right, precision=FULL_PRECISION)
    odd_reduced = odd_blocks - pair_product(left_cross, left_cross) - pair_product(right_fill, right_fill)
    odd_lower = -pair_product(left_cross, fill_block)
    odd_tip = tip_coupling[1::2] - pair_product(tip_side, left_cross) - pair_product(right_side, right_fill)
    odd_rhs = time_rhs[1::2] - jnp.einsum('ibc,ib->ic', left_cross, lifted, precision=FULL_PRECISION) - jnp.einsum('ibc,ib->ic', right_fill, right_lift, precision=FULL_PRECISION)
    schur_block = jnp.diag(tip_prior) + jnp.einsum('tkb,tjb->kj', tip_coupling, tip_coupling, precision=FULL_PRECISION) - jnp.einsum('ibk,ibj->kj', tip_side, tip_side, precision=FULL_PRECISION)
    tip_vec = tip_rhs - jnp.einsum('ibk,ib->k', tip_side, lifted, precision=FULL_PRECISION)
    chol_tip = jnp.linalg.cholesky(schur_block)
    halfway = solve_lower(chol_tip, tip_vec[:, None])
    tip_solution = solve_lower(chol_tip, halfway, True)[:, 0]
    pulled = lifted - jnp.einsum('ibk,k->ib', tip_side, tip_solution, precision=FULL_PRECISION)
    estimate = solve_lower(factor, pulled[:, :, None], True)[:, :, 0]

    def weave(even_part, odd_part):
        return jnp.stack([even_part, odd_part], axis=1).reshape((NT,) + even_part.shape[1:])
    reduced_block = weave(factor, odd_reduced)
    reduced_lower = weave(fill_block, odd_lower)
    reduced_tip = weave(jnp.swapaxes(tip_side, 1, 2), odd_tip)
    time_result = weave(estimate, odd_rhs)
    return (reduced_block, reduced_lower, reduced_tip, time_result, tip_solution)
```

```python
import jax
import jax.numpy as jnp
from jax import lax
from jax.experimental import pallas as pl
from jax.experimental.pallas import tpu as pltpu
from jax.sharding import PartitionSpec as P

R = 2
CAP = 2
T = 128
PANEL = 8
HI = lax.Precision.HIGHEST
VMEM = pl.BlockSpec(memory_space=pltpu.VMEM)


def dot_nn(a, b):
    return lax.dot_general(a, b, (((1,), (0,)), ((), ())), precision=HI, preferred_element_type=jnp.float32)


def dot_nt(a, b):
    return lax.dot_general(a, b, (((1,), (1,)), ((), ())), precision=HI, preferred_element_type=jnp.float32)


def dot_tn(a, b):
    return lax.dot_general(a, b, (((0,), (0,)), ((), ())), precision=HI, preferred_element_type=jnp.float32)


def split3(x):
    h = x.astype(jnp.bfloat16).astype(jnp.float32)
    rest = x - h
    m = rest.astype(jnp.bfloat16).astype(jnp.float32)
    return h, m, rest - m


def panel_gram(rows):
    h, m, l = split3(rows)
    left = jnp.concatenate([part[:, :T] for part in (h, h, m, h, l, m)], axis=0)
    right = jnp.concatenate([h, m, h, l, h, m], axis=0)
    return lax.dot_general(
        left.astype(jnp.bfloat16),
        right.astype(jnp.bfloat16),
        (((0,), (0,)), ((), ())),
        preferred_element_type=jnp.float32,
    )


def factor_tile(work):
    sub = lax.broadcasted_iota(jnp.int32, (PANEL, 2 * T), 0)
    sub_t = lax.broadcasted_iota(jnp.int32, (PANEL, T), 0)
    for p in range(T // PANEL):
        base = p * PANEL
        rows = work[base : base + PANEL, :]
        cols = [
            jnp.broadcast_to(rows[:, base + j : base + j + 1], (PANEL, T)) for j in range(PANEL)
        ]
        scale = jnp.zeros((PANEL, T), jnp.float32)
        for i in range(PANEL):
            pivot = jnp.broadcast_to(cols[i][i : i + 1, :], (PANEL, T))
            root = lax.rsqrt(pivot)
            root = root * (1.5 - 0.5 * pivot * root * root)
            scale = jnp.where(sub_t == i, root, scale)
            if i + 1 < PANEL:
                mult = jnp.where(sub_t > i, cols[i] * (root * root), 0.0)
                mult2 = jnp.concatenate([mult, mult], axis=1)
                rows = rows - mult2 * jnp.broadcast_to(rows[i : i + 1, :], (PANEL, 2 * T))
                for j in range(i + 1, PANEL):
                    cols[j] = cols[j] - mult * jnp.broadcast_to(cols[j][i : i + 1, :], (PANEL, T))
        rows = rows * jnp.concatenate([scale, scale], axis=1)
        work[base : base + PANEL, :] = rows
        if base + PANEL < T:
            work[base + PANEL :, :] = work[base + PANEL :, :] - panel_gram(rows)[base + PANEL :, :]


def eye(n):
    return (
        lax.broadcasted_iota(jnp.int32, (n, n), 0) == lax.broadcasted_iota(jnp.int32, (n, n), 1)
    ).astype(jnp.float32)


def upper_mask(n):
    return lax.broadcasted_iota(jnp.int32, (n, n), 0) <= lax.broadcasted_iota(jnp.int32, (n, n), 1)


def local_kernel(
    rows_ref, tag_ref, label_ref, prior_ref, lower_ref, tip_ref, rhs_ref,
    factor_ref, fill_ref, newlow_ref, side_ref, lift_ref, partblk_ref, parttip_ref, partrhs_ref,
    inv_ref, terms_ref, tlift_ref,
    gram, work, y,
):
    B = prior_ref.shape[1]
    K = tip_ref.shape[1]
    nb = B // T
    tags = tag_ref[...]
    even = label_ref[0:1, 0:1]
    rows = rows_ref[...]
    identity = eye(B)
    chosen = jnp.where(tags == even, rows, 0.0)
    gram[...] = dot_tn(chosen, chosen) + prior_ref[0:1, :] * identity
    inv_ref[...] = jnp.zeros((B, B), jnp.float32)
    factor_ref[...] = jnp.zeros((B, B), jnp.float32)
    upper = upper_mask(T)
    for b in range(nb):
        lo, hi = b * T, (b + 1) * T
        work[:, :T] = gram[lo:hi, lo:hi]
        work[:, T:] = eye(T)
        factor_tile(work)
        inv = jnp.where(upper.T, work[:, T:], 0.0)
        factor_ref[lo:hi, lo:hi] = jnp.where(upper, work[:, :T], 0.0).T
        inv_ref[lo:hi, lo:hi] = inv
        if b > 0:
            inv_ref[lo:hi, :lo] = -dot_nn(inv, dot_nn(factor_ref[lo:hi, :lo], inv_ref[:lo, :lo]))
        if b + 1 < nb:
            upper_rest = dot_nn(inv, gram[lo:hi, hi:])
            gram[hi:, hi:] = gram[hi:, hi:] - dot_tn(upper_rest, upper_rest)
            factor_ref[hi:, lo:hi] = upper_rest.T
    linv = inv_ref[...]
    y[:B, :] = lower_ref[1]
    y[B : B + K, :] = tip_ref[0]
    y[B + K :, :] = jnp.concatenate([rhs_ref[0:1, :], jnp.zeros((7, B), jnp.float32)], axis=0)
    y[...] = dot_nt(y[...], linv)
    fill = dot_nn(linv, lower_ref[0])
    fill_ref[...] = fill
    side = y[B : B + K, :]
    side_ref[...] = side
    lift_ref[...] = y[B + K : B + K + 1, :]
    xt = y[:B, :]
    terms_ref[...] = (
        dot_nt(tip_ref[0], tip_ref[0]) + dot_nt(tip_ref[1], tip_ref[1]) - dot_nt(side, side)
    )
    tlift_ref[...] = dot_nt(y[B + K :, :], side)[0:1, :]
    newlow_ref[...] = -dot_nn(xt, fill)
    back = dot_nt(y[...], xt)
    chosen_odd = jnp.where(tags == even + 1.0, rows, 0.0)
    partblk_ref[...] = dot_tn(chosen_odd, chosen_odd) + prior_ref[1:2, :] * identity - back[:B]
    parttip_ref[...] = tip_ref[1] - back[B : B + K]
    partrhs_ref[...] = rhs_ref[1:2, :] - back[B + K : B + K + 1]


def finish_kernel(fill_ref, side_ref, lift_ref, blk_ref, tip_ref, rhs_ref, oblk, otip, orhs):
    fill = fill_ref[...]
    oblk[...] = blk_ref[...] - dot_tn(fill, fill)
    otip[...] = tip_ref[...] - dot_nn(side_ref[...], fill)
    lift = jnp.concatenate([lift_ref[...]] * 8, axis=0)
    orhs[...] = rhs_ref[...] - dot_nn(lift, fill)[0:1, :]


def tip_kernel(schur_ref, prior_ref, crhs_ref, clift_ref, side_ref, lift_ref, inv_ref, sol_ref, est_ref, work):
    work[:, :T] = schur_ref[...] + prior_ref[...] * eye(T)
    work[:, T:] = eye(T)
    factor_tile(work)
    inv = jnp.where(upper_mask(T).T, work[:, T:], 0.0)
    vec = jnp.concatenate([crhs_ref[...] - clift_ref[...]] * 8, axis=0)
    sol = dot_nn(dot_nt(vec, inv), inv)
    sol_ref[...] = sol[0:1, :]
    lift = jnp.concatenate([lift_ref[...]] * 8, axis=0)
    pulled = lift - dot_nn(sol, side_ref[...])
    est_ref[...] = dot_nn(pulled, inv_ref[...])[0:1, :]


def call(kernel, outs, scratch=()):
    return pl.pallas_call(
        kernel,
        out_shape=[jax.ShapeDtypeStruct(s, jnp.float32) for s in outs],
        scratch_shapes=[pltpu.VMEM(s, jnp.float32) for s in scratch],
        compiler_params=pltpu.CompilerParams(vmem_limit_bytes=56 << 20),
    )


def shifted(value, axis, steps):
    count = lax.axis_size(axis)
    first, last = (max(0, -steps), min(count, count - steps))
    return lax.ppermute(value, axis, [(source, source + steps) for source in range(first, last)])


def local(
    obs_rows, obs_owner, obs_member, prior_diag, lower_coupling, tip_coupling, time_rhs, tip_prior, tip_rhs,
):
    groups = lax.axis_size("tm")
    position = lax.axis_index(("tm", "obs"))
    member_index = lax.axis_index("obs")
    B = prior_diag.shape[1]
    K = tip_coupling.shape[1]
    blocks = obs_rows.shape[0]
    owners = obs_owner[:, 0]
    ordinal = jnp.arange(blocks, dtype=jnp.int32)
    earlier = (owners[:, None] == owners[None, :]) & (ordinal[None, :] < ordinal[:, None])
    slot_rank = jnp.sum(earlier.astype(jnp.int32), axis=1)
    slot_index = owners * CAP + slot_rank
    pick = (jnp.arange(groups * CAP, dtype=jnp.int32)[:, None] == slot_index[None, :]).astype(jnp.float32)
    tagged = jnp.concatenate(
        [obs_rows, jnp.broadcast_to(obs_member.astype(jnp.float32) + 1.0, (blocks, 128))], axis=1
    )
    outgoing = jnp.dot(pick, tagged, precision=HI).reshape(groups, CAP, -1)
    arrived = lax.all_to_all(outgoing, "tm", split_axis=0, concat_axis=0, tiled=True)
    gathered = lax.all_gather(arrived, "obs", axis=0, tiled=True)
    rows_part = gathered[:, :, : R * B].reshape(-1, B)
    tags = jnp.broadcast_to(gathered[:, :, R * B :][:, :, None, :1], gathered.shape[:2] + (R, 1)).reshape(-1, 1)
    label = jnp.full((8, 128), 2 * member_index + 1, jnp.float32)
    masked_lower = jnp.where(position == 0, jnp.zeros_like(lower_coupling[0]), lower_coupling[0])
    lower = jnp.stack([masked_lower, lower_coupling[1]])
    (factor, fill, newlow, side, lift, pblk, ptip, prhs, inv, terms, tlift) = call(
        local_kernel,
        [(B, B), (B, B), (B, B), (K, B), (1, B), (B, B), (K, B), (1, B), (B, B), (K, K), (1, K)],
        [(B, B), (T, 2 * T), (B + K + 8, B)],
    )(rows_part, tags, label, prior_diag, lower, tip_coupling, time_rhs)
    nfill, nside, nlift = shifted((fill, side, lift), ("tm", "obs"), -1)
    schur, slift = lax.psum((terms, tlift), ("tm", "obs"))
    sol, est = call(tip_kernel, [(1, K), (1, B)], [(T, 2 * T)])(
        schur, tip_prior[None, :], tip_rhs[None, :], slift, side, lift, inv
    )
    nblk, ntip, nrhs = call(finish_kernel, [(B, B), (K, B), (1, B)])(nfill, nside, nlift, pblk, ptip, prhs)
    return (
        jnp.stack([factor, nblk]),
        jnp.stack([fill, newlow]),
        jnp.stack([side, ntip]),
        jnp.concatenate([est, nrhs], axis=0),
        sol[0],
    )


def solution(mesh):
    split = ("tm", "obs")
    two, three = P(split, None), P(split, None, None)
    return jax.shard_map(
        local,
        mesh=mesh,
        in_specs=(two, two, two, two, three, three, two, P(), P()),
        out_specs=(three, three, three, two, P()),
        check_vma=False,
    )
```

```python
import jax
import jax.numpy as jnp
from jax import lax
from jax.experimental import pallas as pl
from jax.experimental.pallas import tpu as pltpu
from jax.sharding import PartitionSpec as P

R = 2
CAP = 2
T = 128
PANEL = 8
HI = lax.Precision.HIGHEST
VMEM = pl.BlockSpec(memory_space=pltpu.VMEM)


def dot_nn(a, b):
    return lax.dot_general(a, b, (((1,), (0,)), ((), ())), precision=HI, preferred_element_type=jnp.float32)


def dot_nt(a, b):
    return lax.dot_general(a, b, (((1,), (1,)), ((), ())), precision=HI, preferred_element_type=jnp.float32)


def dot_tn(a, b):
    return lax.dot_general(a, b, (((0,), (0,)), ((), ())), precision=HI, preferred_element_type=jnp.float32)


def split3(x):
    h = x.astype(jnp.bfloat16).astype(jnp.float32)
    rest = x - h
    m = rest.astype(jnp.bfloat16).astype(jnp.float32)
    return h, m, rest - m


def panel_gram(rows):
    h, m, l = split3(rows)
    left = jnp.concatenate([part[:, :T] for part in (h, h, m, h, l, m)], axis=0)
    right = jnp.concatenate([h, m, h, l, h, m], axis=0)
    return lax.dot_general(
        left.astype(jnp.bfloat16),
        right.astype(jnp.bfloat16),
        (((0,), (0,)), ((), ())),
        preferred_element_type=jnp.float32,
    )


def factor_tile(work):
    sub = lax.broadcasted_iota(jnp.int32, (PANEL, 2 * T), 0)
    sub_t = lax.broadcasted_iota(jnp.int32, (PANEL, T), 0)
    for p in range(T // PANEL):
        base = p * PANEL
        rows = work[base : base + PANEL, :]
        cols = [
            jnp.broadcast_to(rows[:, base + j : base + j + 1], (PANEL, T)) for j in range(PANEL)
        ]
        scale = jnp.zeros((PANEL, T), jnp.float32)
        for i in range(PANEL):
            pivot = jnp.broadcast_to(cols[i][i : i + 1, :], (PANEL, T))
            root = lax.rsqrt(pivot)
            root = root * (1.5 - 0.5 * pivot * root * root)
            scale = jnp.where(sub_t == i, root, scale)
            if i + 1 < PANEL:
                mult = jnp.where(sub_t > i, cols[i] * (root * root), 0.0)
                mult2 = jnp.concatenate([mult, mult], axis=1)
                rows = rows - mult2 * jnp.broadcast_to(rows[i : i + 1, :], (PANEL, 2 * T))
                for j in range(i + 1, PANEL):
                    cols[j] = cols[j] - mult * jnp.broadcast_to(cols[j][i : i + 1, :], (PANEL, T))
        rows = rows * jnp.concatenate([scale, scale], axis=1)
        work[base : base + PANEL, :] = rows
        if base + PANEL < T:
            work[base + PANEL :, :] = work[base + PANEL :, :] - panel_gram(rows)[base + PANEL :, :]


def eye(n):
    return (
        lax.broadcasted_iota(jnp.int32, (n, n), 0) == lax.broadcasted_iota(jnp.int32, (n, n), 1)
    ).astype(jnp.float32)


def upper_mask(n):
    return lax.broadcasted_iota(jnp.int32, (n, n), 0) <= lax.broadcasted_iota(jnp.int32, (n, n), 1)


def local_kernel(
    rows_ref, tag_ref, label_ref, prior_ref, lower_ref, tip_ref, rhs_ref,
    factor_ref, low_ref, y_ref, inv_ref, terms_ref, pack_ref,
    gram, work, flat,
):
    B = prior_ref.shape[1]
    K = tip_ref.shape[1]
    nb = B // T
    even = label_ref[0:1, 0:1]
    chosen = jnp.where(tag_ref[...] == even, rows_ref[...], 0.0)
    gram[...] = dot_tn(chosen, chosen) + prior_ref[0:1, :] * eye(B)
    inv_ref[...] = jnp.zeros((B, B), jnp.float32)
    factor_ref[0] = jnp.zeros((B, B), jnp.float32)
    upper = upper_mask(T)
    for b in range(nb):
        lo, hi = b * T, (b + 1) * T
        work[:, :T] = gram[lo:hi, lo:hi]
        work[:, T:] = eye(T)
        factor_tile(work)
        inv = jnp.where(upper.T, work[:, T:], 0.0)
        factor_ref[0, lo:hi, lo:hi] = jnp.where(upper, work[:, :T], 0.0).T
        inv_ref[lo:hi, lo:hi] = inv
        if b > 0:
            inv_ref[lo:hi, :lo] = -dot_nn(inv, dot_nn(factor_ref[0, lo:hi, :lo], inv_ref[:lo, :lo]))
        if b + 1 < nb:
            upper_rest = dot_nn(inv, gram[lo:hi, hi:])
            gram[hi:, hi:] = gram[hi:, hi:] - dot_tn(upper_rest, upper_rest)
            factor_ref[0, hi:, lo:hi] = upper_rest.T
    linv = inv_ref[...]
    low = jnp.where(label_ref[1:2, 0:1] == 0.0, 0.0, lower_ref[0])
    fill = dot_nn(linv, low)
    low_ref[0] = fill
    pack_ref[:B, :] = fill
    y_ref[:B, :] = lower_ref[1]
    y_ref[B : B + K, :] = tip_ref[0]
    y_ref[B + K :, :] = jnp.concatenate([rhs_ref[0:1, :], jnp.zeros((7, B), jnp.float32)], axis=0)
    y_ref[...] = dot_nt(y_ref[...], linv)
    side = y_ref[B : B + K, :]
    pack_ref[B:, :] = y_ref[B:, :]
    flat[:K, :] = (
        dot_nt(tip_ref[0], tip_ref[0]) + dot_nt(tip_ref[1], tip_ref[1]) - dot_nt(side, side)
    )
    flat[K : K + 8, :] = dot_nt(y_ref[B + K :, :], side)
    flat[K + 8 :, :] = jnp.zeros((flat.shape[0] - K - 8, K), jnp.float32)
    chunk = terms_ref.shape[1]
    for i in range(terms_ref.shape[0]):
        terms_ref[i] = flat[i * chunk : (i + 1) * chunk, :] if i * chunk <= K else jnp.zeros((chunk, K), jnp.float32)


def reduce_kernel(x_ref, out_ref, stage, own, full, send_a, recv_a, send_b, recv_b):
    n_tm, n_obs = lax.axis_size("tm"), lax.axis_size("obs")
    n = n_tm * n_obs
    me = lax.axis_index("tm") * n_obs + lax.axis_index("obs")

    def place(k):
        peer = lax.rem(me + k, n)
        return peer, (peer // n_obs, lax.rem(peer, n_obs))

    def scatter(k):
        peer, where = place(k)
        return pltpu.make_async_remote_copy(
            src_ref=x_ref.at[peer], dst_ref=stage.at[k], send_sem=send_a.at[k], recv_sem=recv_a.at[k],
            device_id=where, device_id_type=pl.DeviceIdType.MESH,
        )

    def gather(k):
        _, where = place(k)
        return pltpu.make_async_remote_copy(
            src_ref=own, dst_ref=full.at[k], send_sem=send_b.at[k], recv_sem=recv_b.at[k],
            device_id=where, device_id_type=pl.DeviceIdType.MESH,
        )

    barrier = pltpu.get_barrier_semaphore()

    @pl.loop(1, n)
    def _(k):
        _, where = place(k)
        pl.semaphore_signal(barrier, inc=1, device_id=where, device_id_type=pl.DeviceIdType.MESH)

    pl.semaphore_wait(barrier, n - 1)

    @pl.loop(1, n)
    def _(k):
        scatter(k).start()

    own[...] = x_ref[me]

    @pl.loop(1, n)
    def _(k):
        scatter(k).wait()
        own[...] = own[...] + stage[k]

    @pl.loop(1, n)
    def _(k):
        gather(k).start()

    out_ref[me] = own[...]

    @pl.loop(1, n)
    def _(k):
        gather(k).wait()
        out_ref[lax.rem(me - k + n, n)] = full[k]


def final_kernel(
    rows_ref, tag_ref, label_ref, prior_ref, tip_ref, rhs_ref, y_ref, inv_ref, sum_ref,
    tprior_ref, crhs_ref, next_ref, low_in, blk_in, fill_ref,
    blk_ref, low_ref, otip_ref, res_ref, sol_ref,
    work, flat,
):
    B = prior_ref.shape[1]
    K = tip_ref.shape[1]
    chunk = sum_ref.shape[1]
    for i in range(sum_ref.shape[0]):
        if i * chunk <= K:
            flat[i * chunk : (i + 1) * chunk, :] = sum_ref[i]
    work[:, :T] = flat[:K, :] + tprior_ref[...] * eye(T)
    work[:, T:] = eye(T)
    xt = y_ref[:B, :]
    back = dot_nt(y_ref[...], xt)
    chosen = jnp.where(tag_ref[...] == label_ref[0:1, 0:1] + 1.0, rows_ref[...], 0.0)
    nfill = next_ref[:B, :]
    blk_ref[0] = (
        dot_tn(chosen, chosen) + prior_ref[1:2, :] * eye(B) - back[:B] - dot_tn(nfill, nfill)
    )
    right = dot_nn(next_ref[B:, :], nfill)
    side = y_ref[B : B + K, :]
    otip_ref[0] = side
    otip_ref[1] = tip_ref[1] - back[B : B + K] - right[:K]
    res_ref[1:2, :] = rhs_ref[1:2, :] - back[B + K : B + K + 1] - right[K : K + 1]
    low_ref[0] = -dot_nn(xt, fill_ref[...])
    factor_tile(work)
    inv = jnp.where(upper_mask(T).T, work[:, T:], 0.0)
    vec = jnp.concatenate([crhs_ref[...] - flat[K : K + 1, :]] * 8, axis=0)
    sol = dot_nn(dot_nt(vec, inv), inv)
    sol_ref[...] = sol[0:1, :]
    lift = jnp.concatenate([y_ref[B + K : B + K + 1, :]] * 8, axis=0)
    res_ref[0:1, :] = dot_nn(lift - dot_nn(sol, side), inv_ref[...])[0:1, :]


def call(kernel, outs, scratch=(), in_specs=None, out_specs=None, aliases={}, sems=(), cost=None, grid=None, **params):
    extra = {} if grid is None else {"grid": grid}
    if in_specs is not None:
        extra["in_specs"] = in_specs
    if out_specs is not None:
        extra["out_specs"] = out_specs
    return pl.pallas_call(
        kernel,
        out_shape=[jax.ShapeDtypeStruct(s, jnp.float32) for s in outs],
        scratch_shapes=[pltpu.VMEM(s, jnp.float32) for s in scratch]
        + [pltpu.SemaphoreType.DMA((s,)) for s in sems],
        input_output_aliases=aliases,
        compiler_params=pltpu.CompilerParams(vmem_limit_bytes=56 << 20, **params),
        **extra,
    )


def shifted(value, axis, steps):
    count = lax.axis_size(axis)
    first, last = (max(0, -steps), min(count, count - steps))
    return lax.ppermute(value, axis, [(source, source + steps) for source in range(first, last)])


def local(
    obs_rows, obs_owner, obs_member, prior_diag, lower_coupling, tip_coupling, time_rhs, tip_prior, tip_rhs,
):
    groups = lax.axis_size("tm")
    position = lax.axis_index(("tm", "obs"))
    member_index = lax.axis_index("obs")
    B = prior_diag.shape[1]
    K = tip_coupling.shape[1]
    blocks = obs_rows.shape[0]
    owners = obs_owner[:, 0]
    ordinal = jnp.arange(blocks, dtype=jnp.int32)
    earlier = (owners[:, None] == owners[None, :]) & (ordinal[None, :] < ordinal[:, None])
    slot_rank = jnp.sum(earlier.astype(jnp.int32), axis=1)
    slot_index = owners * CAP + slot_rank
    pick = (jnp.arange(groups * CAP, dtype=jnp.int32)[:, None] == slot_index[None, :]).astype(jnp.float32)
    tagged = jnp.concatenate(
        [obs_rows, jnp.broadcast_to(obs_member.astype(jnp.float32) + 1.0, (blocks, 128))], axis=1
    )
    outgoing = jnp.dot(pick, tagged, precision=HI).reshape(groups, CAP, -1)
    arrived = lax.all_to_all(outgoing, "tm", split_axis=0, concat_axis=0, tiled=True)
    gathered = lax.all_gather(arrived, "obs", axis=0, tiled=True)
    rows_part = gathered[:, :, : R * B].reshape(-1, B)
    tags = jnp.broadcast_to(gathered[:, :, R * B :][:, :, None, :1], gathered.shape[:2] + (R, 1)).reshape(-1, 1)
    label = jnp.concatenate(
        [
            jnp.full((1, 128), 2 * member_index + 1, jnp.float32),
            jnp.full((7, 128), position, jnp.float32),
        ]
    )
    n = groups * lax.axis_size("obs")
    chunk = -(-(K + 1) // n)
    used = -(-(n * chunk + 8) // 8) * 8
    flat_rows = max(used, K + 16)
    first = pl.BlockSpec((1, B, B), lambda i: (0, 0, 0))
    second = pl.BlockSpec((1, B, B), lambda i: (1, 0, 0))

    def whole(shape):
        return pl.BlockSpec(shape, lambda i: (0,) * len(shape))

    rows_args = (rows_part, tags, label, prior_diag)
    wide = (B + K + 8, B)
    block, low, y, inv, terms, pack = call(
        local_kernel,
        [(2, B, B), (2, B, B), wide, (B, B), (n, chunk, K), wide],
        [(B, B), (T, 2 * T), (flat_rows, K)],
        grid=(1,),
        in_specs=[whole(v.shape) for v in (*rows_args, lower_coupling, tip_coupling, time_rhs)],
        out_specs=[first, first, whole(wide), whole((B, B)), whole((n, chunk, K)), whole(wide)],
    )(*rows_args, lower_coupling, tip_coupling, time_rhs)
    following = shifted(pack, ("tm", "obs"), -1)
    total = call(
        reduce_kernel,
        [(n, chunk, K)],
        [(n, chunk, K), (chunk, K), (n, chunk, K)],
        sems=[n, n, n, n],
        in_specs=[VMEM],
        out_specs=[VMEM],
        collective_id=1,
        has_side_effects=True,
    )(terms)[0]
    any_spec = pl.BlockSpec(memory_space=pl.ANY)
    plain = (*rows_args, tip_coupling, time_rhs, y, inv, total, tip_prior[None, :], tip_rhs[None, :], following)
    block, low, tip, result, sol = call(
        final_kernel,
        [(2, B, B), (2, B, B), (2, K, B), (2, B), (1, K)],
        [(T, 2 * T), (flat_rows, K)],
        grid=(1,),
        in_specs=[whole(v.shape) for v in plain] + [any_spec, any_spec, whole((B, B))],
        out_specs=[second, second, whole((2, K, B)), whole((2, B)), whole((1, K))],
        aliases={len(plain): 1, len(plain) + 1: 0},
    )(*plain, low, block, pack[:B])
    return block, low, tip, result, sol[0]


def solution(mesh):
    split = ("tm", "obs")
    two, three = P(split, None), P(split, None, None)
    return jax.shard_map(
        local,
        mesh=mesh,
        in_specs=(two, two, two, two, three, three, two, P(), P()),
        out_specs=(three, three, three, two, P()),
        check_vma=False,
    )
```

```python
import jax
import jax.numpy as jnp
from jax import lax
from jax.experimental import pallas as pl
from jax.experimental.pallas import tpu as pltpu
from jax.sharding import PartitionSpec as P

R = 2
CAP = 2
T = 128
PANEL = 8
HI = lax.Precision.HIGHEST
VMEM = pl.BlockSpec(memory_space=pltpu.VMEM)


def dot_nn(a, b):
    return lax.dot_general(a, b, (((1,), (0,)), ((), ())), precision=HI, preferred_element_type=jnp.float32)


def dot_nt(a, b):
    return lax.dot_general(a, b, (((1,), (1,)), ((), ())), precision=HI, preferred_element_type=jnp.float32)


def dot_tn(a, b):
    return lax.dot_general(a, b, (((0,), (0,)), ((), ())), precision=HI, preferred_element_type=jnp.float32)


def split3(x):
    h = x.astype(jnp.bfloat16).astype(jnp.float32)
    rest = x - h
    m = rest.astype(jnp.bfloat16).astype(jnp.float32)
    return h, m, rest - m


def panel_gram(rows):
    h, m, l = split3(rows)
    left = jnp.concatenate([part[:, :T] for part in (h, h, m, h, l, m)], axis=0)
    right = jnp.concatenate([h, m, h, l, h, m], axis=0)
    return lax.dot_general(
        left.astype(jnp.bfloat16),
        right.astype(jnp.bfloat16),
        (((0,), (0,)), ((), ())),
        preferred_element_type=jnp.float32,
    )


def factor_tile(work):
    sub = lax.broadcasted_iota(jnp.int32, (PANEL, 2 * T), 0)
    sub_t = lax.broadcasted_iota(jnp.int32, (PANEL, T), 0)
    for p in range(T // PANEL):
        base = p * PANEL
        rows = work[base : base + PANEL, :]
        cols = [
            jnp.broadcast_to(rows[:, base + j : base + j + 1], (PANEL, T)) for j in range(PANEL)
        ]
        scale = jnp.zeros((PANEL, T), jnp.float32)
        for i in range(PANEL):
            pivot = jnp.broadcast_to(cols[i][i : i + 1, :], (PANEL, T))
            root = lax.rsqrt(pivot)
            scale = jnp.where(sub_t == i, root, scale)
            if i + 1 < PANEL:
                mult = jnp.where(sub_t > i, cols[i] * (root * root), 0.0)
                mult2 = jnp.concatenate([mult, mult], axis=1)
                rows = rows - mult2 * jnp.broadcast_to(rows[i : i + 1, :], (PANEL, 2 * T))
                for j in range(i + 1, PANEL):
                    cols[j] = cols[j] - mult * jnp.broadcast_to(cols[j][i : i + 1, :], (PANEL, T))
        rows = rows * jnp.concatenate([scale, scale], axis=1)
        work[base : base + PANEL, :] = rows
        if base + PANEL < T:
            work[base + PANEL :, :] = work[base + PANEL :, :] - panel_gram(rows)[base + PANEL :, :]


def eye(n):
    return (
        lax.broadcasted_iota(jnp.int32, (n, n), 0) == lax.broadcasted_iota(jnp.int32, (n, n), 1)
    ).astype(jnp.float32)


def upper_mask(n):
    return lax.broadcasted_iota(jnp.int32, (n, n), 0) <= lax.broadcasted_iota(jnp.int32, (n, n), 1)


def local_kernel(
    rows_ref, tag_ref, label_ref, prior_ref, lower_ref, tip_ref, rhs_ref,
    factor_ref, low_ref, y_ref, inv_ref, terms_ref, pack_ref,
    gram, work, flat,
):
    B = prior_ref.shape[1]
    K = tip_ref.shape[1]
    nb = B // T
    even = label_ref[0:1, 0:1]
    chosen = jnp.where(tag_ref[:, :1] == even, rows_ref[...], 0.0)
    gram[...] = dot_tn(chosen, chosen) + prior_ref[0:1, :] * eye(B)
    inv_ref[...] = jnp.zeros((B, B), jnp.float32)
    factor_ref[0] = jnp.zeros((B, B), jnp.float32)
    upper = upper_mask(T)
    for b in range(nb):
        lo, hi = b * T, (b + 1) * T
        work[:, :T] = gram[lo:hi, lo:hi]
        work[:, T:] = eye(T)
        factor_tile(work)
        inv = jnp.where(upper.T, work[:, T:], 0.0)
        factor_ref[0, lo:hi, lo:hi] = jnp.where(upper, work[:, :T], 0.0).T
        inv_ref[lo:hi, lo:hi] = inv
        if b > 0:
            inv_ref[lo:hi, :lo] = -dot_nn(inv, dot_nn(factor_ref[0, lo:hi, :lo], inv_ref[:lo, :lo]))
        if b + 1 < nb:
            upper_rest = dot_nn(inv, gram[lo:hi, hi:])
            gram[hi:, hi:] = gram[hi:, hi:] - dot_tn(upper_rest, upper_rest)
            factor_ref[0, hi:, lo:hi] = upper_rest.T
    linv = inv_ref[...]
    low = jnp.where(label_ref[1:2, 0:1] == 0.0, 0.0, lower_ref[0])
    fill = dot_nn(linv, low)
    low_ref[0] = fill
    pack_ref[:B, :] = fill
    y_ref[:B, :] = lower_ref[1]
    y_ref[B : B + K, :] = tip_ref[0]
    y_ref[B + K :, :] = jnp.concatenate([rhs_ref[0:1, :], jnp.zeros((7, B), jnp.float32)], axis=0)
    y_ref[...] = dot_nt(y_ref[...], linv)
    side = y_ref[B : B + K, :]
    pack_ref[B:, :] = y_ref[B:, :]
    flat[:K, :] = (
        dot_nt(tip_ref[0], tip_ref[0]) + dot_nt(tip_ref[1], tip_ref[1]) - dot_nt(side, side)
    )
    flat[K : K + 8, :] = dot_nt(y_ref[B + K :, :], side)
    flat[K + 8 :, :] = jnp.zeros((flat.shape[0] - K - 8, K), jnp.float32)
    chunk = terms_ref.shape[1]
    for i in range(terms_ref.shape[0]):
        terms_ref[i] = flat[i * chunk : (i + 1) * chunk, :] if i * chunk <= K else jnp.zeros((chunk, K), jnp.float32)


def reduce_kernel(x_ref, out_ref, stage, own, full, send_a, recv_a, send_b, recv_b):
    n_tm, n_obs = lax.axis_size("tm"), lax.axis_size("obs")
    n = n_tm * n_obs
    me = lax.axis_index("tm") * n_obs + lax.axis_index("obs")

    def place(k):
        peer = lax.rem(me + k, n)
        return peer, (peer // n_obs, lax.rem(peer, n_obs))

    def scatter(k):
        peer, where = place(k)
        return pltpu.make_async_remote_copy(
            src_ref=x_ref.at[peer], dst_ref=stage.at[k], send_sem=send_a.at[k], recv_sem=recv_a.at[k],
            device_id=where, device_id_type=pl.DeviceIdType.MESH,
        )

    def gather(k):
        _, where = place(k)
        return pltpu.make_async_remote_copy(
            src_ref=own, dst_ref=full.at[k], send_sem=send_b.at[k], recv_sem=recv_b.at[k],
            device_id=where, device_id_type=pl.DeviceIdType.MESH,
        )

    barrier = pltpu.get_barrier_semaphore()

    @pl.loop(1, n)
    def _(k):
        _, where = place(k)
        pl.semaphore_signal(barrier, inc=1, device_id=where, device_id_type=pl.DeviceIdType.MESH)

    pl.semaphore_wait(barrier, n - 1)

    @pl.loop(1, n)
    def _(k):
        scatter(k).start()

    own[...] = x_ref[me]

    @pl.loop(1, n)
    def _(k):
        scatter(k).wait()
        own[...] = own[...] + stage[k]

    @pl.loop(1, n)
    def _(k):
        gather(k).start()

    out_ref[me] = own[...]

    @pl.loop(1, n)
    def _(k):
        gather(k).wait()
        out_ref[lax.rem(me - k + n, n)] = full[k]


def tip_kernel(
    rows_ref, tag_ref, label_ref, prior_ref, tip_ref, rhs_ref, y_ref, inv_ref, sum_ref,
    tprior_ref, crhs_ref, fill_ref, low_in,
    low_ref, blk_ref, otip_ref, res_ref, sol_ref,
    work, flat,
):
    B = prior_ref.shape[1]
    K = tip_ref.shape[1]
    chunk = sum_ref.shape[1]
    for i in range(sum_ref.shape[0]):
        if i * chunk <= K:
            flat[i * chunk : (i + 1) * chunk, :] = sum_ref[i]
    work[:, :T] = flat[:K, :] + tprior_ref[...] * eye(T)
    work[:, T:] = eye(T)
    xt = y_ref[:B, :]
    back = dot_nt(y_ref[...], xt)
    chosen = jnp.where(tag_ref[:, :1] == label_ref[0:1, 0:1] + 1.0, rows_ref[...], 0.0)
    blk_ref[...] = dot_tn(chosen, chosen) + prior_ref[1:2, :] * eye(B) - back[:B]
    side = y_ref[B : B + K, :]
    otip_ref[0] = side
    otip_ref[1] = tip_ref[1] - back[B : B + K]
    res_ref[1:2, :] = rhs_ref[1:2, :] - back[B + K : B + K + 1]
    low_ref[0] = -dot_nn(xt, fill_ref[...])
    factor_tile(work)
    inv = jnp.where(upper_mask(T).T, work[:, T:], 0.0)
    vec = jnp.concatenate([crhs_ref[...] - flat[K : K + 1, :]] * 8, axis=0)
    sol = dot_nn(dot_nt(vec, inv), inv)
    sol_ref[...] = sol[0:1, :]
    lift = jnp.concatenate([y_ref[B + K : B + K + 1, :]] * 8, axis=0)
    res_ref[0:1, :] = dot_nn(lift - dot_nn(sol, side), inv_ref[...])[0:1, :]


def finish_kernel(next_ref, part_ref, tip_in, res_in, blk_in, blk_ref, otip_ref, res_ref):
    B = part_ref.shape[1]
    K = tip_in.shape[1]
    nfill = next_ref[:B, :]
    blk_ref[0] = part_ref[...] - dot_tn(nfill, nfill)
    right = dot_nn(next_ref[B:, :], nfill)
    otip_ref[0] = tip_in[0] - right[:K]
    res_ref[0:1, :] = res_in[0:1, :]
    res_ref[1:2, :] = res_in[1:2, :] - right[K : K + 1]


def pack_kernel(rows_ref, owner_ref, member_ref, out_ref):
    groups = out_ref.shape[0]
    blocks, width = rows_ref.shape
    owners = owner_ref[...]
    named = (lax.broadcasted_iota(jnp.int32, (blocks, groups), 1) == owners).astype(jnp.float32)
    before = lax.broadcasted_iota(jnp.int32, (blocks, blocks), 1) < lax.broadcasted_iota(
        jnp.int32, (blocks, blocks), 0
    )
    rank = jnp.sum(dot_nn(before.astype(jnp.float32), named) * named, axis=1, keepdims=True)
    slot = owners.astype(jnp.float32) * CAP + rank
    spots = lax.broadcasted_iota(jnp.int32, (blocks, groups * CAP), 1).astype(jnp.float32)
    pick = (spots == slot).astype(jnp.float32)
    tag = jnp.broadcast_to(member_ref[...].astype(jnp.float32) + 1.0, (blocks, 128))
    rows = dot_tn(pick, rows_ref[...])
    tags = dot_tn(pick, tag)
    for g in range(groups):
        out_ref[g, :, :width] = rows[g * CAP : (g + 1) * CAP, :]
        out_ref[g, :, width:] = tags[g * CAP : (g + 1) * CAP, :]


def route_kernel(x_ref, rows_ref, tags_ref, stage, landed, local_sem, send_a, recv_a, send_b, recv_b):
    groups, n_obs = lax.axis_size("tm"), lax.axis_size("obs")
    t, o = lax.axis_index("tm"), lax.axis_index("obs")
    mesh_id = pl.DeviceIdType.MESH

    def toward(k):
        peer = lax.rem(t + k, groups)
        return pltpu.make_async_remote_copy(
            src_ref=x_ref.at[peer], dst_ref=stage.at[k], send_sem=send_a.at[k], recv_sem=recv_a.at[k],
            device_id=(peer, o), device_id_type=mesh_id,
        )

    def across(k):
        return pltpu.make_async_remote_copy(
            src_ref=stage, dst_ref=landed.at[k], send_sem=send_b.at[k], recv_sem=recv_b.at[k],
            device_id=(t, lax.rem(o + k, n_obs)), device_id_type=mesh_id,
        )

    barrier = pltpu.get_barrier_semaphore()

    @pl.loop(1, groups)
    def _(k):
        pl.semaphore_signal(barrier, inc=1, device_id=(lax.rem(t + k, groups), o), device_id_type=mesh_id)

    @pl.loop(1, n_obs)
    def _(k):
        pl.semaphore_signal(barrier, inc=1, device_id=(t, lax.rem(o + k, n_obs)), device_id_type=mesh_id)

    own = pltpu.make_async_copy(x_ref.at[t], stage.at[0], local_sem.at[0])
    own.start()
    pl.semaphore_wait(barrier, groups + n_obs - 2)

    @pl.loop(1, groups)
    def _(k):
        toward(k).start()

    own.wait()

    @pl.loop(1, groups)
    def _(k):
        toward(k).wait()

    for k in range(1, n_obs):
        across(k).start()
    B = rows_ref.shape[1]
    half = n_obs * groups * CAP
    for k in range(n_obs):
        if k:
            across(k).wait()
        for g in range(groups):
            at = (k * groups + g) * CAP
            piece = landed[k, g] if k else stage[g]
            for r in range(R):
                rows_ref[r * half + at : r * half + at + CAP, :] = piece[:, r * B : (r + 1) * B]
                tags_ref[r * half + at : r * half + at + CAP, :] = piece[:, R * B :]


def call(kernel, outs, scratch=(), in_specs=None, out_specs=None, aliases={}, sems=(), cost=None, grid=None, **params):
    extra = {} if grid is None else {"grid": grid}
    if in_specs is not None:
        extra["in_specs"] = in_specs
    if out_specs is not None:
        extra["out_specs"] = out_specs
    return pl.pallas_call(
        kernel,
        out_shape=[jax.ShapeDtypeStruct(s, jnp.float32) for s in outs],
        scratch_shapes=[pltpu.VMEM(s, jnp.float32) for s in scratch]
        + [pltpu.SemaphoreType.DMA((s,)) for s in sems],
        input_output_aliases=aliases,
        cost_estimate=cost,
        compiler_params=pltpu.CompilerParams(vmem_limit_bytes=56 << 20, **params),
        **extra,
    )


def shifted(value, axis, steps):
    count = lax.axis_size(axis)
    first, last = (max(0, -steps), min(count, count - steps))
    return lax.ppermute(value, axis, [(source, source + steps) for source in range(first, last)])


def local(
    obs_rows, obs_owner, obs_member, prior_diag, lower_coupling, tip_coupling, time_rhs, tip_prior, tip_rhs,
):
    groups = lax.axis_size("tm")
    position = lax.axis_index(("tm", "obs"))
    member_index = lax.axis_index("obs")
    B = prior_diag.shape[1]
    K = tip_coupling.shape[1]
    members = lax.axis_size("obs")
    width = R * B + 128
    outgoing = call(pack_kernel, [(groups, CAP, width)])(obs_rows, obs_owner, obs_member)[0]
    count = members * groups * CAP * R
    rows_part, tags = call(
        route_kernel,
        [(count, B), (count, 128)],
        [(groups, CAP, width), (members, groups, CAP, width)],
        sems=[1, groups, groups, members, members],
        in_specs=[VMEM],
        out_specs=[VMEM, VMEM],
        collective_id=2,
        has_side_effects=True,
    )(outgoing)
    label = jnp.concatenate(
        [
            jnp.full((1, 128), 2 * member_index + 1, jnp.float32),
            jnp.full((7, 128), position, jnp.float32),
        ]
    )
    n = groups * lax.axis_size("obs")
    chunk = -(-(K + 1) // n)
    used = -(-(n * chunk + 8) // 8) * 8
    flat_rows = max(used, K + 16)
    first = pl.BlockSpec((1, B, B), lambda i: (0, 0, 0))
    second = pl.BlockSpec((1, B, B), lambda i: (1, 0, 0))

    def whole(shape):
        return pl.BlockSpec(shape, lambda i: (0,) * len(shape))

    rows_args = (rows_part, tags, label, prior_diag)
    wide = (B + K + 8, B)
    block, low, y, inv, terms, pack = call(
        local_kernel,
        [(2, B, B), (2, B, B), wide, (B, B), (n, chunk, K), wide],
        [(B, B), (T, 2 * T), (flat_rows, K)],
        grid=(1,),
        in_specs=[whole(v.shape) for v in (*rows_args, lower_coupling, tip_coupling, time_rhs)],
        out_specs=[first, first, whole(wide), whole((B, B)), whole((n, chunk, K)), whole(wide)],
    )(*rows_args, lower_coupling, tip_coupling, time_rhs)
    total = call(
        reduce_kernel,
        [(n, chunk, K)],
        [(n, chunk, K), (chunk, K), (n, chunk, K)],
        sems=[n, n, n, n],
        in_specs=[VMEM],
        out_specs=[VMEM],
        collective_id=1,
        has_side_effects=True,
    )(terms)[0]
    pack_late, total_late = lax.optimization_barrier((pack, total))
    following = shifted(pack_late, ("tm", "obs"), -1)
    any_spec = pl.BlockSpec(memory_space=pl.ANY)
    plain = (*rows_args, tip_coupling, time_rhs, y, inv, total_late, tip_prior[None, :], tip_rhs[None, :])
    low, part, tip, result, sol = call(
        tip_kernel,
        [(2, B, B), (B, B), (2, K, B), (2, B), (1, K)],
        [(T, 2 * T), (flat_rows, K)],
        grid=(1,),
        in_specs=[whole(v.shape) for v in plain] + [whole((B, B)), any_spec],
        out_specs=[second, whole((B, B)), whole((2, K, B)), whole((2, B)), whole((1, K))],
        aliases={len(plain) + 1: 0},
        cost=pl.CostEstimate(flops=10**9, bytes_accessed=40 * 10**6, transcendentals=0),
    )(*plain, pack_late, low)
    block, tip, result = call(
        finish_kernel,
        [(2, B, B), (2, K, B), (2, B)],
        grid=(1,),
        in_specs=[whole(wide), whole((B, B)), pl.BlockSpec((1, K, B), lambda i: (1, 0, 0)), whole((2, B)), any_spec],
        out_specs=[second, pl.BlockSpec((1, K, B), lambda i: (1, 0, 0)), whole((2, B))],
        aliases={2: 1, 4: 0},
    )(following, part, tip, result, block)
    return block, low, tip, result, sol[0]


def solution(mesh):
    split = ("tm", "obs")
    two, three = P(split, None), P(split, None, None)
    return jax.shard_map(
        local,
        mesh=mesh,
        in_specs=(two, two, two, two, three, three, two, P(), P()),
        out_specs=(three, three, three, two, P()),
        check_vma=False,
    )
```

```python
import jax
import jax.numpy as jnp
from jax import lax
from jax.experimental import pallas as pl
from jax.experimental.pallas import tpu as pltpu
from jax.sharding import PartitionSpec as P

R = 2
CAP = 2
T = 128
PANEL = 8
HI = lax.Precision.HIGHEST
VMEM = pl.BlockSpec(memory_space=pltpu.VMEM)


def dot_nn(a, b):
    return lax.dot_general(a, b, (((1,), (0,)), ((), ())), precision=HI, preferred_element_type=jnp.float32)


def dot_nt(a, b):
    return lax.dot_general(a, b, (((1,), (1,)), ((), ())), precision=HI, preferred_element_type=jnp.float32)


def dot_tn(a, b):
    return lax.dot_general(a, b, (((0,), (0,)), ((), ())), precision=HI, preferred_element_type=jnp.float32)


def split3(x):
    h = x.astype(jnp.bfloat16).astype(jnp.float32)
    rest = x - h
    m = rest.astype(jnp.bfloat16).astype(jnp.float32)
    return h, m, rest - m


def panel_gram(rows):
    h, m, l = split3(rows)
    left = jnp.concatenate([part[:, :T] for part in (h, h, m, h, l, m)], axis=0)
    right = jnp.concatenate([h, m, h, l, h, m], axis=0)
    return lax.dot_general(
        left.astype(jnp.bfloat16),
        right.astype(jnp.bfloat16),
        (((0,), (0,)), ((), ())),
        preferred_element_type=jnp.float32,
    )


def factor_tile(work):
    sub = lax.broadcasted_iota(jnp.int32, (PANEL, 2 * T), 0)
    sub_t = lax.broadcasted_iota(jnp.int32, (PANEL, T), 0)
    for p in range(T // PANEL):
        base = p * PANEL
        rows = work[base : base + PANEL, :]
        cols = [
            jnp.broadcast_to(rows[:, base + j : base + j + 1], (PANEL, T)) for j in range(PANEL)
        ]
        scale = jnp.zeros((PANEL, T), jnp.float32)
        for i in range(PANEL):
            pivot = jnp.broadcast_to(cols[i][i : i + 1, :], (PANEL, T))
            root = lax.rsqrt(pivot)
            scale = jnp.where(sub_t == i, root, scale)
            if i + 1 < PANEL:
                mult = jnp.where(sub_t > i, cols[i] * (root * root), 0.0)
                mult2 = jnp.concatenate([mult, mult], axis=1)
                rows = rows - mult2 * jnp.broadcast_to(rows[i : i + 1, :], (PANEL, 2 * T))
                for j in range(i + 1, PANEL):
                    cols[j] = cols[j] - mult * jnp.broadcast_to(cols[j][i : i + 1, :], (PANEL, T))
        rows = rows * jnp.concatenate([scale, scale], axis=1)
        work[base : base + PANEL, :] = rows
        if base + PANEL < T:
            work[base + PANEL :, :] = work[base + PANEL :, :] - panel_gram(rows)[base + PANEL :, :]


def eye(n):
    return (
        lax.broadcasted_iota(jnp.int32, (n, n), 0) == lax.broadcasted_iota(jnp.int32, (n, n), 1)
    ).astype(jnp.float32)


def upper_mask(n):
    return lax.broadcasted_iota(jnp.int32, (n, n), 0) <= lax.broadcasted_iota(jnp.int32, (n, n), 1)


def local_kernel(
    rows_ref, tag_ref, prior_ref, lower_ref, tip_ref, rhs_ref,
    factor_ref, low_ref, y_ref, inv_ref, terms_ref, pack_ref,
    gram, work, flat,
):
    B = prior_ref.shape[1]
    K = tip_ref.shape[1]
    nb = B // T
    even = (2 * lax.axis_index("obs") + 1).astype(jnp.float32)
    chosen = jnp.where(tag_ref[:, :1] == even, rows_ref[...], 0.0)
    gram[...] = dot_tn(chosen, chosen) + prior_ref[0:1, :] * eye(B)
    inv_ref[...] = jnp.zeros((B, B), jnp.float32)
    factor_ref[0] = jnp.zeros((B, B), jnp.float32)
    upper = upper_mask(T)
    for b in range(nb):
        lo, hi = b * T, (b + 1) * T
        work[:, :T] = gram[lo:hi, lo:hi]
        work[:, T:] = eye(T)
        factor_tile(work)
        inv = jnp.where(upper.T, work[:, T:], 0.0)
        factor_ref[0, lo:hi, lo:hi] = jnp.where(upper, work[:, :T], 0.0).T
        inv_ref[lo:hi, lo:hi] = inv
        if b > 0:
            inv_ref[lo:hi, :lo] = -dot_nn(inv, dot_nn(factor_ref[0, lo:hi, :lo], inv_ref[:lo, :lo]))
        if b + 1 < nb:
            upper_rest = dot_nn(inv, gram[lo:hi, hi:])
            gram[hi:, hi:] = gram[hi:, hi:] - dot_tn(upper_rest, upper_rest)
            factor_ref[0, hi:, lo:hi] = upper_rest.T
    linv = inv_ref[...]
    position = lax.axis_index("tm") * lax.axis_size("obs") + lax.axis_index("obs")
    low = jnp.where(position == 0, 0.0, lower_ref[0])
    fill = dot_nn(linv, low)
    low_ref[0] = fill
    pack_ref[:B, :] = fill
    y_ref[:B, :] = lower_ref[1]
    y_ref[B : B + K, :] = tip_ref[0]
    y_ref[B + K :, :] = jnp.concatenate([rhs_ref[0:1, :], jnp.zeros((7, B), jnp.float32)], axis=0)
    y_ref[...] = dot_nt(y_ref[...], linv)
    side = y_ref[B : B + K, :]
    pack_ref[B:, :] = y_ref[B:, :]
    flat[:K, :] = (
        dot_nt(tip_ref[0], tip_ref[0]) + dot_nt(tip_ref[1], tip_ref[1]) - dot_nt(side, side)
    )
    flat[K : K + 8, :] = dot_nt(y_ref[B + K :, :], side)
    flat[K + 8 :, :] = jnp.zeros((flat.shape[0] - K - 8, K), jnp.float32)
    chunk = terms_ref.shape[1]
    for i in range(terms_ref.shape[0]):
        terms_ref[i] = flat[i * chunk : (i + 1) * chunk, :] if i * chunk <= K else jnp.zeros((chunk, K), jnp.float32)


def reduce_kernel(x_ref, out_ref, stage, own, full, send_a, recv_a, send_b, recv_b):
    n_tm, n_obs = lax.axis_size("tm"), lax.axis_size("obs")
    n = n_tm * n_obs
    me = lax.axis_index("tm") * n_obs + lax.axis_index("obs")

    def place(k):
        peer = lax.rem(me + k, n)
        return peer, (peer // n_obs, lax.rem(peer, n_obs))

    def scatter(k):
        peer, where = place(k)
        return pltpu.make_async_remote_copy(
            src_ref=x_ref.at[peer], dst_ref=stage.at[k], send_sem=send_a.at[k], recv_sem=recv_a.at[k],
            device_id=where, device_id_type=pl.DeviceIdType.MESH,
        )

    def gather(k):
        _, where = place(k)
        return pltpu.make_async_remote_copy(
            src_ref=own, dst_ref=full.at[k], send_sem=send_b.at[k], recv_sem=recv_b.at[k],
            device_id=where, device_id_type=pl.DeviceIdType.MESH,
        )

    barrier = pltpu.get_barrier_semaphore()

    @pl.loop(1, n)
    def _(k):
        _, where = place(k)
        pl.semaphore_signal(barrier, inc=1, device_id=where, device_id_type=pl.DeviceIdType.MESH)

    pl.semaphore_wait(barrier, n - 1)

    @pl.loop(1, n)
    def _(k):
        scatter(k).start()

    own[...] = x_ref[me]

    @pl.loop(1, n)
    def _(k):
        scatter(k).wait()
        own[...] = own[...] + stage[k]

    @pl.loop(1, n)
    def _(k):
        gather(k).start()

    out_ref[me] = own[...]

    @pl.loop(1, n)
    def _(k):
        gather(k).wait()
        out_ref[lax.rem(me - k + n, n)] = full[k]


def tip_kernel(
    rows_ref, tag_ref, prior_ref, tip_ref, rhs_ref, y_ref, inv_ref, sum_ref,
    tprior_ref, crhs_ref, fill_ref, low_in,
    low_ref, blk_ref, otip_ref, res_ref, sol_ref,
    work, flat,
):
    B = prior_ref.shape[1]
    K = tip_ref.shape[1]
    chunk = sum_ref.shape[1]
    for i in range(sum_ref.shape[0]):
        if i * chunk <= K:
            flat[i * chunk : (i + 1) * chunk, :] = sum_ref[i]
    work[:, :T] = flat[:K, :] + tprior_ref[...] * eye(T)
    work[:, T:] = eye(T)
    xt = y_ref[:B, :]
    back = dot_nt(y_ref[...], xt)
    odd = (2 * lax.axis_index("obs") + 2).astype(jnp.float32)
    chosen = jnp.where(tag_ref[:, :1] == odd, rows_ref[...], 0.0)
    blk_ref[...] = dot_tn(chosen, chosen) + prior_ref[1:2, :] * eye(B) - back[:B]
    side = y_ref[B : B + K, :]
    otip_ref[0] = side
    otip_ref[1] = tip_ref[1] - back[B : B + K]
    res_ref[1:2, :] = rhs_ref[1:2, :] - back[B + K : B + K + 1]
    low_ref[0] = -dot_nn(xt, fill_ref[...])
    factor_tile(work)
    inv = jnp.where(upper_mask(T).T, work[:, T:], 0.0)
    vec = jnp.concatenate([crhs_ref[...] - flat[K : K + 1, :]] * 8, axis=0)
    sol = dot_nn(dot_nt(vec, inv), inv)
    sol_ref[...] = sol[0:1, :]
    lift = jnp.concatenate([y_ref[B + K : B + K + 1, :]] * 8, axis=0)
    res_ref[0:1, :] = dot_nn(lift - dot_nn(sol, side), inv_ref[...])[0:1, :]


def finish_kernel(next_ref, part_ref, tip_in, res_in, blk_in, blk_ref, otip_ref, res_ref):
    B = part_ref.shape[1]
    K = tip_in.shape[1]
    nfill = next_ref[:B, :]
    blk_ref[0] = part_ref[...] - dot_tn(nfill, nfill)
    right = dot_nn(next_ref[B:, :], nfill)
    otip_ref[0] = tip_in[0] - right[:K]
    res_ref[0:1, :] = res_in[0:1, :]
    res_ref[1:2, :] = res_in[1:2, :] - right[K : K + 1]


def pack_kernel(rows_ref, owner_ref, member_ref, out_ref):
    groups = out_ref.shape[0]
    blocks, width = rows_ref.shape
    owners = owner_ref[...]
    named = (lax.broadcasted_iota(jnp.int32, (groups, blocks), 0) == owners).astype(jnp.float32)
    before = lax.broadcasted_iota(jnp.int32, (blocks, blocks), 0) < lax.broadcasted_iota(
        jnp.int32, (blocks, blocks), 1
    )
    rank = jnp.sum(dot_nn(named, before.astype(jnp.float32)) * named, axis=0, keepdims=True)
    slot = owners.astype(jnp.float32) * CAP + rank
    spots = lax.broadcasted_iota(jnp.int32, (groups * CAP, blocks), 0).astype(jnp.float32)
    pick = (spots == slot).astype(jnp.float32)
    rows = dot_nn(pick, rows_ref[...])
    tag = jnp.sum(pick * (member_ref[...].astype(jnp.float32) + 1.0), axis=1, keepdims=True)
    tags = jnp.broadcast_to(tag, (groups * CAP, 128))
    for g in range(groups):
        out_ref[g, :, :width] = rows[g * CAP : (g + 1) * CAP, :]
        out_ref[g, :, width:] = tags[g * CAP : (g + 1) * CAP, :]


def route_kernel(x_ref, rows_ref, tags_ref, stage, landed, local_sem, send_a, recv_a, send_b, recv_b):
    groups, n_obs = lax.axis_size("tm"), lax.axis_size("obs")
    t, o = lax.axis_index("tm"), lax.axis_index("obs")
    mesh_id = pl.DeviceIdType.MESH

    def toward(k):
        peer = lax.rem(t + k, groups)
        return pltpu.make_async_remote_copy(
            src_ref=x_ref.at[peer], dst_ref=stage.at[k], send_sem=send_a.at[k], recv_sem=recv_a.at[k],
            device_id=(peer, o), device_id_type=mesh_id,
        )

    def across(k):
        return pltpu.make_async_remote_copy(
            src_ref=stage, dst_ref=landed.at[k], send_sem=send_b.at[k], recv_sem=recv_b.at[k],
            device_id=(t, lax.rem(o + k, n_obs)), device_id_type=mesh_id,
        )

    barrier = pltpu.get_barrier_semaphore()

    @pl.loop(1, groups)
    def _(k):
        pl.semaphore_signal(barrier, inc=1, device_id=(lax.rem(t + k, groups), o), device_id_type=mesh_id)

    @pl.loop(1, n_obs)
    def _(k):
        pl.semaphore_signal(barrier, inc=1, device_id=(t, lax.rem(o + k, n_obs)), device_id_type=mesh_id)

    own = pltpu.make_async_copy(x_ref.at[t], stage.at[0], local_sem.at[0])
    own.start()
    pl.semaphore_wait(barrier, groups + n_obs - 2)

    @pl.loop(1, groups)
    def _(k):
        toward(k).start()

    own.wait()

    @pl.loop(1, groups)
    def _(k):
        toward(k).wait()

    for k in range(1, n_obs):
        across(k).start()
    B = rows_ref.shape[1]
    half = n_obs * groups * CAP
    for k in range(n_obs):
        if k:
            across(k).wait()
        for g in range(groups):
            at = (k * groups + g) * CAP
            piece = landed[k, g] if k else stage[g]
            for r in range(R):
                rows_ref[r * half + at : r * half + at + CAP, :] = piece[:, r * B : (r + 1) * B]
                tags_ref[r * half + at : r * half + at + CAP, :] = piece[:, R * B :]


def call(kernel, outs, scratch=(), in_specs=None, out_specs=None, aliases={}, sems=(), cost=None, grid=None, **params):
    extra = {} if grid is None else {"grid": grid}
    if in_specs is not None:
        extra["in_specs"] = in_specs
    if out_specs is not None:
        extra["out_specs"] = out_specs
    return pl.pallas_call(
        kernel,
        out_shape=[jax.ShapeDtypeStruct(s, jnp.float32) for s in outs],
        scratch_shapes=[pltpu.VMEM(s, jnp.float32) for s in scratch]
        + [pltpu.SemaphoreType.DMA((s,)) for s in sems],
        input_output_aliases=aliases,
        cost_estimate=cost,
        compiler_params=pltpu.CompilerParams(vmem_limit_bytes=56 << 20, **params),
        **extra,
    )


def shifted(value, axis, steps):
    count = lax.axis_size(axis)
    first, last = (max(0, -steps), min(count, count - steps))
    return lax.ppermute(value, axis, [(source, source + steps) for source in range(first, last)])


def local(
    obs_rows, obs_owner, obs_member, prior_diag, lower_coupling, tip_coupling, time_rhs, tip_prior, tip_rhs,
):
    groups = lax.axis_size("tm")
    B = prior_diag.shape[1]
    K = tip_coupling.shape[1]
    members = lax.axis_size("obs")
    width = R * B + 128
    outgoing = call(pack_kernel, [(groups, CAP, width)])(obs_rows, obs_owner.reshape(1, -1), obs_member.reshape(1, -1))[0]
    count = members * groups * CAP * R
    rows_part, tags = call(
        route_kernel,
        [(count, B), (count, 128)],
        [(groups, CAP, width), (members, groups, CAP, width)],
        sems=[1, groups, groups, members, members],
        in_specs=[VMEM],
        out_specs=[VMEM, VMEM],
        collective_id=2,
        has_side_effects=True,
    )(outgoing)
    n = groups * lax.axis_size("obs")
    chunk = -(-(K + 1) // n)
    used = -(-(n * chunk + 8) // 8) * 8
    flat_rows = max(used, K + 16)
    first = pl.BlockSpec((1, B, B), lambda i: (0, 0, 0))
    second = pl.BlockSpec((1, B, B), lambda i: (1, 0, 0))

    def whole(shape):
        return pl.BlockSpec(shape, lambda i: (0,) * len(shape))

    rows_args = (rows_part, tags, prior_diag)
    wide = (B + K + 8, B)
    block, low, y, inv, terms, pack = call(
        local_kernel,
        [(2, B, B), (2, B, B), wide, (B, B), (n, chunk, K), wide],
        [(B, B), (T, 2 * T), (flat_rows, K)],
        grid=(1,),
        in_specs=[whole(v.shape) for v in (*rows_args, lower_coupling, tip_coupling, time_rhs)],
        out_specs=[first, first, whole(wide), whole((B, B)), whole((n, chunk, K)), whole(wide)],
    )(*rows_args, lower_coupling, tip_coupling, time_rhs)
    total = call(
        reduce_kernel,
        [(n, chunk, K)],
        [(n, chunk, K), (chunk, K), (n, chunk, K)],
        sems=[n, n, n, n],
        in_specs=[VMEM],
        out_specs=[VMEM],
        collective_id=1,
        has_side_effects=True,
    )(terms)[0]
    pack_late, total_late = lax.optimization_barrier((pack, total))
    following = shifted(pack_late, ("tm", "obs"), -1)
    any_spec = pl.BlockSpec(memory_space=pl.ANY)
    plain = (*rows_args, tip_coupling, time_rhs, y, inv, total_late, tip_prior[None, :], tip_rhs[None, :])
    low, part, tip, result, sol = call(
        tip_kernel,
        [(2, B, B), (B, B), (2, K, B), (2, B), (1, K)],
        [(T, 2 * T), (flat_rows, K)],
        grid=(1,),
        in_specs=[whole(v.shape) for v in plain] + [whole((B, B)), any_spec],
        out_specs=[second, whole((B, B)), whole((2, K, B)), whole((2, B)), whole((1, K))],
        aliases={len(plain) + 1: 0},
        cost=pl.CostEstimate(flops=10**9, bytes_accessed=40 * 10**6, transcendentals=0),
    )(*plain, pack_late, low)
    block, tip, result = call(
        finish_kernel,
        [(2, B, B), (2, K, B), (2, B)],
        grid=(1,),
        in_specs=[whole(wide), whole((B, B)), pl.BlockSpec((1, K, B), lambda i: (1, 0, 0)), whole((2, B)), any_spec],
        out_specs=[second, pl.BlockSpec((1, K, B), lambda i: (1, 0, 0)), whole((2, B))],
        aliases={2: 1, 4: 0},
    )(following, part, tip, result, block)
    return block, low, tip, result, sol[0]


def solution(mesh):
    split = ("tm", "obs")
    two, three = P(split, None), P(split, None, None)
    return jax.shard_map(
        local,
        mesh=mesh,
        in_specs=(two, two, two, two, three, three, two, P(), P()),
        out_specs=(three, three, three, two, P()),
        check_vma=False,
    )
```
